32 devices in a mesh: groups: 2 (over x), tile: 16 (over z, y, core).
Axes of the slice: x: 2, y: 2, z: 4, core: 2. Of those that a mesh axis runs over, the one named last changes fastest.
Arguments:
- grid_tokens: bfloat16 [16384, 512], P(('groups', 'tile')), parts along dimension 0, may hold values from -220 to 220
- obs_features: bfloat16 [65536, 128], P(('groups', 'tile')), parts along dimension 0, may hold values from -45 to 45
- w_obs: bfloat16 [128, 512], replicated, may hold values from -0.5 to 0.5
- b_obs: float32 [512], replicated, may hold values from -4 to 4
- w_query: bfloat16 [512, 512], replicated, may hold values from -0.25 to 0.25
- w_key: bfloat16 [512, 512], replicated, may hold values from -0.25 to 0.25
- w_value: bfloat16 [512, 512], replicated, may hold values from -0.25 to 0.25
- w_out: bfloat16 [512, 512], replicated, may hold values from -0.25 to 0.25
- block_lists: int32 [128, 32], P('groups'), parts along dimension 0, may hold values from 0 to 511, as said below
- block_counts: int32 [128], P('groups'), parts along dimension 0, may hold values from 24 to 32, as said below
- block_position: int32 [1024], P('groups'), parts along dimension 0, may hold values from 0 to 511, as said below
- proc_order: int32 [128], P('groups'), parts along dimension 0, may hold values from 0 to 63, each once
Outputs:
- arranged: bfloat16 [16384, 512], P(('groups', 'tile')), parts along dimension 0
The draws below stay inside these ranges and needn't reach their ends.
There are 2 independent parts, one for each index of `groups`. The reference program is written for one: setup_inputs(seed, part) draws one part's arguments, and reference() takes and returns one part's arrays. A program takes and returns all parts, laid end to end along the dimension named above; an argument that names none is the same for every part. Nothing has to cross between parts.
Inputs may be any that keep to these rules, and one draw needn't show every extreme that they name: `block_lists`: over the entries below block_counts of the 4 tiles t of one device (t // 4 equal), at most 16 name blocks whose storage position // 32 is any one device; in every draw some device has exactly 16 from some device. `block_counts`: some tile uses all 32 entries. `block_position`: A permutation of the storage positions.
All inputs are finite; a program needn't handle non-finite values.
Results may differ from the reference program's by a relative error of at most 0.012.
The reference program's roundings to bfloat16 on the way count: a program that leaves them out, or rounds other values in their place, can miss the bound.
Values may be sent and summed in bfloat16 or wider, within the bound.
A program may use at most 128 MiB of HBM per device.

```python
import math
import jax
import jax.numpy as jnp
from jax import lax

D = 512
FEAT = 128
HEADS = 8
BLOCK = 64
NSEL = 32
TILE_ROWS = 128
TILES_DEV = 4
OB_DEV = 32
TILES = 64
NBLK = 512
PIECE = 8
N_TILE = 16


def plan_blocks(key):
    position = jax.random.permutation(jax.random.fold_in(key, 101), NBLK).astype(jnp.int32)
    inverse = jnp.argsort(position).astype(jnp.int32)
    capacity = max(2, 2 * TILES_DEV * NSEL // N_TILE)
    entries = TILES_DEV * NSEL
    groups_needed = entries // capacity
    owner_keys = jax.random.split(jax.random.fold_in(key, 102), N_TILE)
    owner_perm = jax.vmap(lambda sub: jax.random.permutation(sub, N_TILE))(owner_keys)[:, :groups_needed]
    owner_dev = jnp.repeat(owner_perm.astype(jnp.int32), capacity, axis=1)
    local_blk = jax.random.randint(jax.random.fold_in(key, 103), (N_TILE, entries), 0, OB_DEV).astype(jnp.int32)
    blocks = jnp.take(inverse, owner_dev * OB_DEV + local_blk, axis=0).reshape(TILES, NSEL)
    shuffle_keys = jax.random.split(jax.random.fold_in(key, 104), TILES)
    shuffle = jax.vmap(lambda sub: jax.random.permutation(sub, NSEL))(shuffle_keys).astype(jnp.int32)
    lists = jnp.take_along_axis(blocks, shuffle, axis=1).astype(jnp.int32)
    counts = jax.random.randint(jax.random.fold_in(key, 105), (TILES,), 3 * NSEL // 4, NSEL + 1).astype(jnp.int32)
    full_tile = jax.random.randint(jax.random.fold_in(key, 106), (), 0, TILES)
    counts = jnp.where(jnp.arange(TILES) == full_tile, NSEL, counts).astype(jnp.int32)
    return (lists, counts, position)


def draw_block_lists(key, part):
    return plan_blocks(key)[0]


def draw_block_counts(key, part):
    return plan_blocks(key)[1]


def draw_block_position(key, part):
    return plan_blocks(key)[2]


def draw_grid_tokens(key, part):
    row_total = TILES * TILE_ROWS
    values = jnp.clip(jax.random.normal(jax.random.fold_in(key, 205), (row_total, D), jnp.float32), -6.0, 6.0)
    return values.astype(jnp.bfloat16)


def draw_obs_features(key, part):
    row_total = NBLK * BLOCK
    dev_rows = OB_DEV * BLOCK
    device_of_row = jnp.arange(row_total, dtype=jnp.int32) // dev_rows
    rise_pos = device_of_row.astype(jnp.float32)[:, None] / float(max(N_TILE - 1, 1))
    jitter = jnp.exp(jax.random.uniform(jax.random.fold_in(key, 306), (N_TILE, 1), jnp.float32, math.log(0.6), math.log(1.2)))
    dev_center = jax.random.uniform(jax.random.fold_in(key, 307), (N_TILE, FEAT), jnp.float32, -3.0, 3.0)
    blk_scale = jnp.exp(jax.random.uniform(jax.random.fold_in(key, 308), (NBLK, 1), jnp.float32, math.log(0.25), math.log(2.5)))
    spread = jnp.exp(jax.random.uniform(jax.random.fold_in(key, 301), (1, FEAT), jnp.float32, math.log(0.5), math.log(2.0)))
    row_jitter = jnp.repeat(jitter, dev_rows, axis=0)
    row_center = jnp.repeat(dev_center, dev_rows, axis=0)
    row_scale = jnp.repeat(blk_scale, BLOCK, axis=0)
    rise = 1.0 + 2.0 * rise_pos
    center = row_center
    noise = jnp.clip(jax.random.normal(jax.random.fold_in(key, 305), (row_total, FEAT), jnp.float32), -4.0, 4.0)
    values = rise * row_jitter * (center + row_scale * spread * noise)
    return jnp.clip(values, -45.0, 45.0).astype(jnp.bfloat16)


def gaussian(key, extent, scale, bound, kind=jnp.bfloat16):
    values = jax.random.normal(key, extent, jnp.float32) * scale
    return jnp.minimum(jnp.maximum(values, -bound), bound).astype(kind)


def setup_inputs(seed: int = 0, part: int = 0) -> dict:
    arg_keys = jax.random.split(jax.random.key(seed), 13)
    part_splits = jax.random.split(jax.random.fold_in(arg_keys[12], part), 13)
    return {
        "grid_tokens": draw_grid_tokens(jax.random.fold_in(jax.random.fold_in(arg_keys[12], part), 71), part),
        "obs_features": draw_obs_features(jax.random.fold_in(jax.random.fold_in(arg_keys[12], part), 71), part),
        "w_obs": gaussian(arg_keys[2], (FEAT, D), FEAT ** -0.5, 0.5),
        "b_obs": gaussian(arg_keys[3], (D,), 1.0, 4.0, jnp.float32),
        "w_query": gaussian(arg_keys[4], (D, D), D ** -0.5, 0.25),
        "w_key": gaussian(arg_keys[5], (D, D), D ** -0.5, 0.25),
        "w_value": gaussian(arg_keys[6], (D, D), D ** -0.5, 0.25),
        "w_out": gaussian(arg_keys[7], (D, D), D ** -0.5, 0.25),
        "block_lists": draw_block_lists(jax.random.fold_in(jax.random.fold_in(arg_keys[12], part), 71), part),
        "block_counts": draw_block_counts(jax.random.fold_in(jax.random.fold_in(arg_keys[12], part), 71), part),
        "block_position": draw_block_position(jax.random.fold_in(jax.random.fold_in(arg_keys[12], part), 71), part),
        "proc_order": jax.random.permutation(part_splits[11], TILES).astype(jnp.int32),
    }


def embed_rows(feats, feat_mean, feat_rstd, w_obs, b_obs):
    normed = ((feats.astype(jnp.float32) - feat_mean) * feat_rstd).astype(jnp.bfloat16)
    hidden = jnp.dot(normed, w_obs, preferred_element_type=jnp.float32) + b_obs
    return jax.nn.gelu(hidden, approximate=True).astype(jnp.bfloat16)

def reference(grid_tokens, obs_features, w_obs, b_obs, w_query, w_key, w_value, w_out, block_lists, block_counts, block_position, proc_order):
    obs_wide = obs_features.astype(jnp.float32)
    obs_total = obs_wide.shape[0]
    feat_mean = lax.optimization_barrier(jnp.sum(obs_wide, axis=0)) / obs_total
    second = lax.optimization_barrier(jnp.sum(obs_wide * obs_wide, axis=0)) / obs_total
    feat_rstd = lax.rsqrt(second - feat_mean * feat_mean + 1e-05)
    embedded = embed_rows(obs_features, feat_mean, feat_rstd, w_obs, b_obs)
    key_all = jnp.dot(embedded, w_key, preferred_element_type=jnp.float32).astype(jnp.bfloat16).reshape(NBLK, BLOCK, D)
    value_all = jnp.dot(embedded, w_value, preferred_element_type=jnp.float32).astype(jnp.bfloat16).reshape(NBLK, BLOCK, D)
    query_all = jnp.dot(grid_tokens, w_query, preferred_element_type=jnp.float32).astype(jnp.bfloat16).reshape(TILES, TILE_ROWS, D)
    head_dim = D // HEADS
    scale = 1.0 / head_dim ** 0.5

    def one_tile(items):
        query_tile, blocks, used = items
        spots = jnp.take(block_position, blocks, axis=0)
        key_tile = jnp.take(key_all, spots, axis=0).reshape(NSEL * BLOCK, HEADS, head_dim).astype(jnp.float32)
        value_tile = jnp.take(value_all, spots, axis=0).reshape(NSEL * BLOCK, HEADS, head_dim).astype(jnp.float32)
        query_wide = query_tile.reshape(TILE_ROWS, HEADS, head_dim).astype(jnp.float32)
        keymask = jnp.repeat(jnp.arange(NSEL, dtype=jnp.int32) < used, BLOCK)
        scores = jnp.einsum('qhd,khd->hqk', query_wide, key_tile) * scale
        scores = jnp.where(keymask[None, None, :], scores, jnp.float32(-1e+30))
        peak = lax.optimization_barrier(jnp.max(scores, axis=-1, keepdims=True))
        expo = jnp.exp(scores - peak)
        totals = lax.optimization_barrier(jnp.sum(expo, axis=-1))
        weights_bf = lax.optimization_barrier(expo.astype(jnp.bfloat16)).astype(jnp.float32)
        mixed = jnp.einsum('hqk,khd->qhd', weights_bf, value_tile)
        mixed = mixed / jnp.transpose(totals, (1, 0))[:, :, None]
        return mixed.reshape(TILE_ROWS, D).astype(jnp.bfloat16)
    attended = lax.map(one_tile, (query_all, block_lists, block_counts))
    encoded = jnp.dot(attended.reshape(TILES * TILE_ROWS, D), w_out, preferred_element_type=jnp.float32).astype(jnp.bfloat16)
    encoded = encoded.reshape(TILES, N_TILE, PIECE, D)
    placed = jnp.take(encoded, proc_order, axis=0)
    return jnp.transpose(placed, (1, 0, 2, 3)).reshape(TILES * TILE_ROWS, D)
```

```python
import functools

import jax
import jax.numpy as jnp
from jax import lax
from jax.experimental import pallas as pl
from jax.experimental.pallas import tpu as pltpu
from jax.sharding import PartitionSpec as P

HEADS = 8
BLOCK = 64
NSEL = 32
TILE_ROWS = 128
CHUNK = 512
NEG = -1e30


def attend_kernel(
    pick_ref,
    count_ref,
    grid_ref,
    blocks_ref,
    mean_ref,
    rstd_ref,
    w_obs_ref,
    b_obs_ref,
    w_query_ref,
    w_key_ref,
    w_value_ref,
    w_out_ref,
    out_ref,
    raw,
    keys,
    values,
    copy_sem,
):
    tile = pl.program_id(0)
    tiles = pl.num_programs(0)
    key_span = NSEL * BLOCK
    width = grid_ref.shape[1]
    pair = 2 * (width // HEADS)

    def fetch(which):
        slot = lax.rem(which, 2)

        def one(j, carry):
            spot = pick_ref[which * NSEL + j]
            pltpu.make_async_copy(
                blocks_ref.at[pl.ds(spot * BLOCK, BLOCK), :],
                raw.at[slot, pl.ds(j * BLOCK, BLOCK), :],
                copy_sem.at[slot],
            ).start()
            return carry

        lax.fori_loop(0, NSEL, one, 0)

    @pl.when(tile == 0)
    def _():
        fetch(tile)

    slot = lax.rem(tile, 2)
    pltpu.make_async_copy(
        blocks_ref.at[pl.ds(0, key_span), :], raw.at[slot], copy_sem.at[slot]
    ).wait()

    @pl.when(tile + 1 < tiles)
    def _():
        fetch(tile + 1)

    for start in range(0, key_span, CHUNK):
        rows = pl.ds(start, CHUNK)
        feats = raw[slot, rows, :].astype(jnp.float32)
        normed = ((feats - mean_ref[...]) * rstd_ref[...]).astype(jnp.bfloat16)
        hidden = jnp.dot(normed, w_obs_ref[...], preferred_element_type=jnp.float32)
        hidden = hidden + b_obs_ref[...]
        embedded = jax.nn.gelu(hidden, approximate=True).astype(jnp.bfloat16)
        keys[rows, :] = jnp.dot(
            embedded, w_key_ref[...], preferred_element_type=jnp.float32
        ).astype(jnp.bfloat16)
        values[rows, :] = jnp.dot(
            embedded, w_value_ref[...], preferred_element_type=jnp.float32
        ).astype(jnp.bfloat16)

    queries = jnp.dot(
        grid_ref[...], w_query_ref[...], preferred_element_type=jnp.float32
    ).astype(jnp.bfloat16)
    queries = queries * jnp.bfloat16(1.0 / (width // HEADS) ** 0.5)
    used = count_ref[tile] * BLOCK
    key_index = lax.broadcasted_iota(jnp.int32, (1, key_span), 1)
    bias = jnp.where(key_index < used, 0.0, NEG).astype(jnp.float32)
    lane = lax.broadcasted_iota(jnp.int32, (TILE_ROWS, pair), 1)
    first = lane < pair // 2
    zero = jnp.zeros((), jnp.bfloat16)
    parts = []
    for p in range(HEADS // 2):
        columns = slice(p * pair, (p + 1) * pair)
        q = queries[:, columns]
        both = jnp.concatenate([jnp.where(first, q, zero), jnp.where(first, zero, q)], axis=0)
        scores = lax.dot_general(
            both,
            keys[:, columns],
            (((1,), (1,)), ((), ())),
            preferred_element_type=jnp.float32,
        )
        scores = scores + bias
        peak = jnp.max(scores, axis=-1, keepdims=True)
        expo = jnp.exp(scores - peak)
        totals = jnp.sum(expo, axis=-1, keepdims=True)
        mixed = jnp.dot(
            expo.astype(jnp.bfloat16), values[:, columns], preferred_element_type=jnp.float32
        )
        mixed = mixed / totals
        parts.append(
            jnp.where(first, mixed[:TILE_ROWS], mixed[TILE_ROWS:]).astype(jnp.bfloat16)
        )
    attended = jnp.concatenate(parts, axis=1)
    out_ref[...] = jnp.dot(
        attended, w_out_ref[...], preferred_element_type=jnp.float32
    ).astype(jnp.bfloat16)


def attend(
    pick, counts, grid_tokens, blocks, mean, rstd, w_obs, b_obs, w_query, w_key, w_value, w_out
):
    rows, width = grid_tokens.shape
    feat = blocks.shape[1]
    key_span = NSEL * BLOCK

    def whole(shape):
        return pl.BlockSpec(shape, lambda t, *_: (0, 0))

    square = whole((width, width))
    return pl.pallas_call(
        attend_kernel,
        grid_spec=pltpu.PrefetchScalarGridSpec(
            num_scalar_prefetch=2,
            grid=(rows // TILE_ROWS,),
            in_specs=[
                pl.BlockSpec((TILE_ROWS, width), lambda t, *_: (t, 0)),
                pl.BlockSpec(memory_space=pl.ANY),
                whole((1, feat)),
                whole((1, feat)),
                whole((feat, width)),
                whole((1, width)),
                square,
                square,
                square,
                square,
            ],
            out_specs=pl.BlockSpec((TILE_ROWS, width), lambda t, *_: (t, 0)),
            scratch_shapes=[
                pltpu.VMEM((2, key_span, feat), jnp.bfloat16),
                pltpu.VMEM((key_span, width), jnp.bfloat16),
                pltpu.VMEM((key_span, width), jnp.bfloat16),
                pltpu.SemaphoreType.DMA((2,)),
            ],
        ),
        out_shape=jax.ShapeDtypeStruct((rows, width), jnp.bfloat16),
        compiler_params=pltpu.CompilerParams(dimension_semantics=("arbitrary",)),
        cost_estimate=pl.CostEstimate(
            flops=12_000_000_000, bytes_accessed=6_000_000, transcendentals=12_000_000
        ),
    )(
        pick,
        counts,
        grid_tokens,
        blocks,
        mean[None],
        rstd[None],
        w_obs,
        b_obs[None],
        w_query,
        w_key,
        w_value,
        w_out,
    )


def exchange(obs_features, block_lists, block_counts, block_position, tile_count, own_index):
    obs_blocks = obs_features.shape[0] // BLOCK
    tile_local = block_lists.shape[0] // tile_count
    entry_count = tile_local * NSEL
    capacity = max(2, 2 * entry_count // tile_count)
    spots = jnp.take(block_position, block_lists, axis=0)
    is_valid = jnp.arange(NSEL, dtype=jnp.int32)[None, :] < block_counts[:, None]
    owner_dev = (spots // obs_blocks).reshape(tile_count, entry_count)
    local_blk = (spots % obs_blocks).reshape(tile_count, entry_count)
    valid_rows = is_valid.reshape(tile_count, entry_count)
    entry_order = jnp.arange(entry_count, dtype=jnp.int32)
    earlier = (
        (owner_dev[:, :, None] == owner_dev[:, None, :])
        & valid_rows[:, None, :]
        & (entry_order[None, :] < entry_order[:, None])[None, :, :]
    )
    slot_rank = jnp.sum(earlier.astype(jnp.int32), axis=2)
    mine = valid_rows & (owner_dev == own_index)
    slot_ids = jnp.arange(capacity, dtype=jnp.int32)
    hits = mine[:, None, :] & (slot_rank[:, None, :] == slot_ids[None, :, None])
    slot_block = jnp.sum(jnp.where(hits, local_blk[:, None, :], 0), axis=2)
    my_owner = lax.dynamic_index_in_dim(owner_dev, own_index, 0, keepdims=False)
    my_rank = lax.dynamic_index_in_dim(slot_rank, own_index, 0, keepdims=False)
    my_valid = lax.dynamic_index_in_dim(valid_rows, own_index, 0, keepdims=False)
    pick = jnp.where(my_valid, my_owner * capacity + my_rank, 0)
    raw_blocks = obs_features.reshape(obs_blocks, BLOCK, obs_features.shape[1])
    incoming = lax.all_to_all(
        jnp.take(raw_blocks, slot_block, axis=0), "tile", split_axis=0, concat_axis=0, tiled=True
    )
    return incoming.reshape(tile_count * capacity * BLOCK, obs_features.shape[1]), pick


def local(
    grid_tokens,
    obs_features,
    w_obs,
    b_obs,
    w_query,
    w_key,
    w_value,
    w_out,
    block_lists,
    block_counts,
    block_position,
    proc_order,
):
    tile_count = lax.axis_size("tile")
    own_index = lax.axis_index("tile")
    tile_local = grid_tokens.shape[0] // TILE_ROWS
    width = grid_tokens.shape[1]
    obs_wide = obs_features.astype(jnp.float32)
    first_sum, second_sum = lax.psum(
        (jnp.sum(obs_wide, axis=0), jnp.sum(obs_wide * obs_wide, axis=0)), "tile"
    )
    obs_total = obs_features.shape[0] * tile_count
    feat_mean = first_sum / obs_total
    feat_rstd = lax.rsqrt(second_sum / obs_total - feat_mean * feat_mean + 1e-05)
    my_counts = lax.dynamic_slice_in_dim(block_counts, own_index * tile_local, tile_local)
    if tile_count <= 16:
        blocks = lax.all_gather(obs_features, "tile", axis=0, tiled=True)
        my_lists = lax.dynamic_slice_in_dim(block_lists, own_index * tile_local, tile_local)
        pick = jnp.take(block_position, my_lists.reshape(-1), axis=0)
    else:
        blocks, pick = exchange(
            obs_features, block_lists, block_counts, block_position, tile_count, own_index
        )
    encoded = attend(
        pick,
        my_counts,
        grid_tokens,
        blocks,
        feat_mean,
        feat_rstd,
        w_obs,
        b_obs,
        w_query,
        w_key,
        w_value,
        w_out,
    )
    outgoing = encoded.reshape(tile_local, tile_count, TILE_ROWS // tile_count, width)
    arrived = lax.all_to_all(outgoing, "tile", split_axis=1, concat_axis=0, tiled=True)
    arrived = arrived.reshape(tile_count * tile_local, TILE_ROWS // tile_count, width)
    return jnp.take(arrived, proc_order, axis=0).reshape(
        tile_count * tile_local * (TILE_ROWS // tile_count), width
    )


def solution(mesh):
    in_specs = (
        P(("groups", "tile"), None),
        P(("groups", "tile"), None),
        P(),
        P(),
        P(),
        P(),
        P(),
        P(),
        P("groups", None),
        P("groups"),
        P("groups"),
        P("groups"),
    )
    out_specs = P(("groups", "tile"), None)
    return jax.shard_map(local, mesh=mesh, in_specs=in_specs, out_specs=out_specs, check_vma=False)
```

```python
import functools

import jax
import jax.numpy as jnp
from jax import lax
from jax.experimental import pallas as pl
from jax.experimental.pallas import tpu as pltpu
from jax.sharding import PartitionSpec as P

HEADS = 8
BLOCK = 64
NSEL = 32
TILE_ROWS = 128
CHUNK = 512
NEG = -1e30


def attend_kernel(
    pick_ref,
    count_ref,
    grid_ref,
    blocks_ref,
    mean_ref,
    rstd_ref,
    w_obs_ref,
    b_obs_ref,
    w_query_ref,
    w_key_ref,
    w_value_ref,
    w_out_ref,
    out_ref,
    raw,
    keys,
    values,
    copy_sem,
):
    tile = pl.program_id(0)
    tiles = pl.num_programs(0)
    key_span = NSEL * BLOCK
    width = grid_ref.shape[1]
    pair = 2 * (width // HEADS)

    def fetch(which):
        slot = lax.rem(which, 2)

        def one(j, carry):
            spot = pick_ref[which * NSEL + j]
            pltpu.make_async_copy(
                blocks_ref.at[pl.ds(spot * BLOCK, BLOCK), :],
                raw.at[slot, pl.ds(j * BLOCK, BLOCK), :],
                copy_sem.at[slot],
            ).start()
            return carry

        lax.fori_loop(0, NSEL, one, 0)

    @pl.when(tile == 0)
    def _():
        fetch(tile)

    slot = lax.rem(tile, 2)
    pltpu.make_async_copy(
        blocks_ref.at[pl.ds(0, key_span), :], raw.at[slot], copy_sem.at[slot]
    ).wait()

    @pl.when(tile + 1 < tiles)
    def _():
        fetch(tile + 1)

    for start in range(0, key_span, CHUNK):
        rows = pl.ds(start, CHUNK)
        feats = raw[slot, rows, :].astype(jnp.float32)
        normed = ((feats - mean_ref[...]) * rstd_ref[...]).astype(jnp.bfloat16)
        hidden = jnp.dot(normed, w_obs_ref[...], preferred_element_type=jnp.float32)
        hidden = hidden + b_obs_ref[...]
        embedded = jax.nn.gelu(hidden, approximate=True).astype(jnp.bfloat16)
        keys[rows, :] = jnp.dot(
            embedded, w_key_ref[...], preferred_element_type=jnp.float32
        ).astype(jnp.bfloat16)
        values[rows, :] = jnp.dot(
            embedded, w_value_ref[...], preferred_element_type=jnp.float32
        ).astype(jnp.bfloat16)

    queries = jnp.dot(
        grid_ref[...], w_query_ref[...], preferred_element_type=jnp.float32
    ).astype(jnp.bfloat16)
    queries = queries * jnp.bfloat16(1.0 / (width // HEADS) ** 0.5)
    used = count_ref[tile] * BLOCK
    key_index = lax.broadcasted_iota(jnp.int32, (1, key_span), 1)
    bias = jnp.where(key_index < used, 0.0, NEG).astype(jnp.float32)
    lane = lax.broadcasted_iota(jnp.int32, (TILE_ROWS, pair), 1)
    first = lane < pair // 2
    zero = jnp.zeros((), jnp.bfloat16)
    parts = []
    for p in range(HEADS // 2):
        columns = slice(p * pair, (p + 1) * pair)
        q = queries[:, columns]
        both = jnp.concatenate([jnp.where(first, q, zero), jnp.where(first, zero, q)], axis=0)
        scores = lax.dot_general(
            both,
            keys[:, columns],
            (((1,), (1,)), ((), ())),
            preferred_element_type=jnp.float32,
        )
        scores = scores + bias
        peak = jnp.max(scores, axis=-1, keepdims=True)
        expo = jnp.exp(scores - peak)
        totals = jnp.sum(expo, axis=-1, keepdims=True)
        mixed = jnp.dot(
            expo.astype(jnp.bfloat16), values[:, columns], preferred_element_type=jnp.float32
        )
        mixed = mixed / totals
        parts.append(
            jnp.where(first, mixed[:TILE_ROWS], mixed[TILE_ROWS:]).astype(jnp.bfloat16)
        )
    attended = jnp.concatenate(parts, axis=1)
    encoded = jnp.dot(
        attended, w_out_ref[...], preferred_element_type=jnp.float32
    ).astype(jnp.bfloat16)
    out_ref[...] = encoded.reshape(out_ref.shape)


def attend(
    tile_count,
    pick,
    counts,
    grid_tokens,
    blocks,
    mean,
    rstd,
    w_obs,
    b_obs,
    w_query,
    w_key,
    w_value,
    w_out,
):
    rows, width = grid_tokens.shape
    piece = TILE_ROWS // tile_count
    feat = blocks.shape[1]
    key_span = NSEL * BLOCK

    def whole(shape):
        return pl.BlockSpec(shape, lambda t, *_: (0, 0))

    square = whole((width, width))
    return pl.pallas_call(
        attend_kernel,
        grid_spec=pltpu.PrefetchScalarGridSpec(
            num_scalar_prefetch=2,
            grid=(rows // TILE_ROWS,),
            in_specs=[
                pl.BlockSpec((TILE_ROWS, width), lambda t, *_: (t, 0)),
                pl.BlockSpec(memory_space=pl.ANY),
                whole((1, feat)),
                whole((1, feat)),
                whole((feat, width)),
                whole((1, width)),
                square,
                square,
                square,
                square,
            ],
            out_specs=pl.BlockSpec((tile_count, 1, piece, width), lambda t, *_: (0, t, 0, 0)),
            scratch_shapes=[
                pltpu.VMEM((2, key_span, feat), jnp.bfloat16),
                pltpu.VMEM((key_span, width), jnp.bfloat16),
                pltpu.VMEM((key_span, width), jnp.bfloat16),
                pltpu.SemaphoreType.DMA((2,)),
            ],
        ),
        out_shape=jax.ShapeDtypeStruct(
            (tile_count, rows // TILE_ROWS, piece, width), jnp.bfloat16
        ),
        compiler_params=pltpu.CompilerParams(dimension_semantics=("arbitrary",)),
        cost_estimate=pl.CostEstimate(
            flops=12_000_000_000, bytes_accessed=6_000_000, transcendentals=12_000_000
        ),
    )(
        pick,
        counts,
        grid_tokens,
        blocks,
        mean,
        rstd,
        w_obs,
        b_obs[None],
        w_query,
        w_key,
        w_value,
        w_out,
    )


MESH = pl.DeviceIdType.MESH


def greet_all(me, count):
    barrier = pltpu.get_barrier_semaphore()

    def one(k, carry):
        peer = lax.rem(me + k, count)
        pl.semaphore_signal(barrier, inc=1, device_id={"tile": peer}, device_id_type=MESH)
        return carry

    lax.fori_loop(1, count, one, 0)
    pl.semaphore_wait(barrier, count - 1)


def gather_kernel(
    lines, obs_ref, all_ref, mean_ref, rstd_ref, part, parts, sends, recvs, part_sends, part_recvs, own_sem
):
    count = 4 * lines
    me = lax.axis_index("tile")
    z, y, c = me // 4, lax.rem(me // 2, 2), lax.rem(me, 2)
    rows = obs_ref.shape[0]

    def index(zz, yy, cc):
        return (zz * 2 + yy) * 2 + cc

    def place(block):
        return all_ref.at[pl.ds(pl.multiple_of(block * rows, rows), rows), :]

    def send(source, block, way, target):
        return pltpu.make_async_remote_copy(
            src_ref=source,
            dst_ref=place(block),
            send_sem=sends.at[way, block],
            recv_sem=recvs.at[block],
            device_id={"tile": target},
            device_id_type=MESH,
        )

    down, up = index(z - 1, y, c), index(z + 1, y, c)
    across, beside = index(z, 1 - y, c), index(z, y, 1 - c)

    greet_all(me, count)
    own = pltpu.make_async_copy(obs_ref, place(me), own_sem)

    @pl.when(z > 0)
    def _():
        send(obs_ref, me, 0, down).start()

    @pl.when(z < lines - 1)
    def _():
        send(obs_ref, me, 1, up).start()

    send(obs_ref, me, 2, across).start()
    send(obs_ref, me, 3, beside).start()
    own.start()

    feats = obs_ref[...].astype(jnp.float32)
    part[...] = jnp.zeros_like(part)
    part[0:1, :] = jnp.sum(feats, axis=0, keepdims=True)
    part[1:2, :] = jnp.sum(feats * feats, axis=0, keepdims=True)
    parts[pl.ds(me, 1)] = part[...][None]

    for hop in range(1, lines + 1):
        if hop < lines:
            from_up, from_down = index(z + hop, y, c), index(z - hop, y, c)

            @pl.when(z + hop < lines)
            def _():
                send(place(from_up), from_up, 3, beside).wait_recv()

                @pl.when(z > 0)
                def _():
                    send(place(from_up), from_up, 0, down).start()

                send(place(from_up), from_up, 2, across).start()
                send(place(from_up), from_up, 3, beside).start()

            @pl.when(z - hop >= 0)
            def _():
                send(place(from_down), from_down, 3, beside).wait_recv()

                @pl.when(z < lines - 1)
                def _():
                    send(place(from_down), from_down, 1, up).start()

                send(place(from_down), from_down, 2, across).start()
                send(place(from_down), from_down, 3, beside).start()

        if hop == 1:

            def share(k, carry):
                peer = lax.rem(me + k, count)
                pltpu.make_async_remote_copy(
                    src_ref=part,
                    dst_ref=parts.at[me],
                    send_sem=part_sends.at[k],
                    recv_sem=part_recvs.at[me],
                    device_id={"tile": peer},
                    device_id_type=MESH,
                ).start()
                return carry

            lax.fori_loop(1, count, share, 0)

        far = hop - 1
        for sign in (1, -1) if far else (1,):
            other = index(z + sign * far, 1 - y, c)

            @pl.when((z + sign * far >= 0) & (z + sign * far < lines))
            def _():
                send(place(other), other, 3, beside).wait_recv()
                send(place(other), other, 3, beside).start()

    def gathered(k, carry):
        peer = lax.rem(me + k, count)
        copy = pltpu.make_async_remote_copy(
            src_ref=part,
            dst_ref=parts.at[peer],
            send_sem=part_sends.at[k],
            recv_sem=part_recvs.at[peer],
            device_id={"tile": peer},
            device_id_type=MESH,
        )
        copy.wait_send()
        copy.wait_recv()
        return carry

    lax.fori_loop(1, count, gathered, 0)
    sums = jnp.sum(parts[...], axis=0)
    total = rows * count
    mean = sums[0:1, :] / total
    mean_ref[...] = mean
    rstd_ref[...] = lax.rsqrt(sums[1:2, :] / total - mean * mean + 1e-05)

    for zz in range(lines):
        for yy in range(2):
            theirs, mine = index(zz, yy, 1 - c), index(zz, yy, c)
            send(place(theirs), theirs, 3, beside).wait_recv()
            send(place(mine), mine, 3, beside).wait_send()
        held = index(zz, y, c)
        send(place(held), held, 2, across).wait_send()

        @pl.when((zz >= z) & (z > 0))
        def _():
            send(place(held), held, 0, down).wait_send()

        @pl.when((zz <= z) & (z < lines - 1))
        def _():
            send(place(held), held, 1, up).wait_send()

    own.wait()


def gather_blocks(obs_features, tile_count):
    rows, feat = obs_features.shape
    small = jax.ShapeDtypeStruct((1, feat), jnp.float32)
    vmem = pl.BlockSpec(memory_space=pltpu.VMEM)
    return pl.pallas_call(
        functools.partial(gather_kernel, tile_count // 4),
        out_shape=(
            jax.ShapeDtypeStruct((tile_count * rows, feat), obs_features.dtype),
            small,
            small,
        ),
        in_specs=[vmem],
        out_specs=(pl.BlockSpec(memory_space=pl.ANY), vmem, vmem),
        scratch_shapes=[
            pltpu.VMEM((8, feat), jnp.float32),
            pltpu.VMEM((tile_count, 8, feat), jnp.float32),
            pltpu.SemaphoreType.DMA((4, tile_count)),
            pltpu.SemaphoreType.DMA((tile_count,)),
            pltpu.SemaphoreType.DMA((tile_count,)),
            pltpu.SemaphoreType.DMA((tile_count,)),
            pltpu.SemaphoreType.DMA,
        ],
        compiler_params=pltpu.CompilerParams(collective_id=0, has_side_effects=True),
    )(obs_features)


def scatter_kernel(count, order_ref, encoded_ref, out_ref, arrived, sends, recvs):
    me = lax.axis_index("tile")
    tile_local = encoded_ref.shape[1]
    greet_all(me, count)

    def copy(source, peer, k):
        return pltpu.make_async_remote_copy(
            src_ref=encoded_ref.at[peer],
            dst_ref=arrived.at[pl.ds(source * tile_local, tile_local)],
            send_sem=sends.at[k],
            recv_sem=recvs.at[source],
            device_id={"tile": peer},
            device_id_type=MESH,
        )

    def start(k, carry):
        copy(me, lax.rem(me + k, count), k).start()
        return carry

    def finish(k, carry):
        peer = lax.rem(me + k, count)
        copy(peer, peer, k).wait_send()
        copy(peer, peer, k).wait_recv()
        return carry

    lax.fori_loop(1, count, start, 0)
    arrived[pl.ds(me * tile_local, tile_local)] = encoded_ref[me]
    lax.fori_loop(1, count, finish, 0)

    def arrange(j, carry):
        out_ref[pl.ds(j, 1)] = arrived[pl.ds(order_ref[j], 1)]
        return carry

    lax.fori_loop(0, count * tile_local, arrange, 0, unroll=8)


def scatter(encoded, proc_order):
    count, tile_local, piece, width = encoded.shape
    vmem = pl.BlockSpec(memory_space=pltpu.VMEM)
    shape = (count * tile_local, piece, width)
    return pl.pallas_call(
        functools.partial(scatter_kernel, count),
        out_shape=jax.ShapeDtypeStruct(shape, encoded.dtype),
        in_specs=[pl.BlockSpec(memory_space=pltpu.SMEM), vmem],
        out_specs=vmem,
        scratch_shapes=[
            pltpu.VMEM(shape, encoded.dtype),
            pltpu.SemaphoreType.DMA((count,)),
            pltpu.SemaphoreType.DMA((count,)),
        ],
        compiler_params=pltpu.CompilerParams(collective_id=1, has_side_effects=True),
    )(proc_order, encoded).reshape(count * tile_local * piece, width)


def exchange(obs_features, block_lists, block_counts, block_position, tile_count, own_index):
    obs_blocks = obs_features.shape[0] // BLOCK
    tile_local = block_lists.shape[0] // tile_count
    entry_count = tile_local * NSEL
    capacity = max(2, 2 * entry_count // tile_count)
    spots = jnp.take(block_position, block_lists, axis=0)
    is_valid = jnp.arange(NSEL, dtype=jnp.int32)[None, :] < block_counts[:, None]
    owner_dev = (spots // obs_blocks).reshape(tile_count, entry_count)
    local_blk = (spots % obs_blocks).reshape(tile_count, entry_count)
    valid_rows = is_valid.reshape(tile_count, entry_count)
    entry_order = jnp.arange(entry_count, dtype=jnp.int32)
    earlier = (
        (owner_dev[:, :, None] == owner_dev[:, None, :])
        & valid_rows[:, None, :]
        & (entry_order[None, :] < entry_order[:, None])[None, :, :]
    )
    slot_rank = jnp.sum(earlier.astype(jnp.int32), axis=2)
    mine = valid_rows & (owner_dev == own_index)
    slot_ids = jnp.arange(capacity, dtype=jnp.int32)
    hits = mine[:, None, :] & (slot_rank[:, None, :] == slot_ids[None, :, None])
    slot_block = jnp.sum(jnp.where(hits, local_blk[:, None, :], 0), axis=2)
    my_owner = lax.dynamic_index_in_dim(owner_dev, own_index, 0, keepdims=False)
    my_rank = lax.dynamic_index_in_dim(slot_rank, own_index, 0, keepdims=False)
    my_valid = lax.dynamic_index_in_dim(valid_rows, own_index, 0, keepdims=False)
    pick = jnp.where(my_valid, my_owner * capacity + my_rank, 0)
    raw_blocks = obs_features.reshape(obs_blocks, BLOCK, obs_features.shape[1])
    incoming = lax.all_to_all(
        jnp.take(raw_blocks, slot_block, axis=0), "tile", split_axis=0, concat_axis=0, tiled=True
    )
    return incoming.reshape(tile_count * capacity * BLOCK, obs_features.shape[1]), pick


def local(
    grid_tokens,
    obs_features,
    w_obs,
    b_obs,
    w_query,
    w_key,
    w_value,
    w_out,
    block_lists,
    block_counts,
    block_position,
    proc_order,
):
    tile_count = lax.axis_size("tile")
    own_index = lax.axis_index("tile")
    tile_local = grid_tokens.shape[0] // TILE_ROWS
    width = grid_tokens.shape[1]
    my_counts = lax.dynamic_slice_in_dim(block_counts, own_index * tile_local, tile_local)
    near = tile_count <= 16 and tile_count % 4 == 0
    if near:
        blocks, feat_mean, feat_rstd = gather_blocks(obs_features, tile_count)
        my_lists = lax.dynamic_slice_in_dim(block_lists, own_index * tile_local, tile_local)
        pick = jnp.take(block_position, my_lists.reshape(-1), axis=0)
    else:
        obs_wide = obs_features.astype(jnp.float32)
        first_sum, second_sum = lax.psum(
            (
                jnp.sum(obs_wide, axis=0, keepdims=True),
                jnp.sum(obs_wide * obs_wide, axis=0, keepdims=True),
            ),
            "tile",
        )
        obs_total = obs_features.shape[0] * tile_count
        feat_mean = first_sum / obs_total
        feat_rstd = lax.rsqrt(second_sum / obs_total - feat_mean * feat_mean + 1e-05)
        blocks, pick = exchange(
            obs_features, block_lists, block_counts, block_position, tile_count, own_index
        )
    encoded = attend(
        tile_count if near else 1,
        pick,
        my_counts,
        grid_tokens,
        blocks,
        feat_mean,
        feat_rstd,
        w_obs,
        b_obs,
        w_query,
        w_key,
        w_value,
        w_out,
    )
    if near:
        return scatter(encoded, proc_order)
    outgoing = encoded.reshape(tile_local, tile_count, TILE_ROWS // tile_count, width)
    arrived = lax.all_to_all(outgoing, "tile", split_axis=1, concat_axis=0, tiled=True)
    arrived = arrived.reshape(tile_count * tile_local, TILE_ROWS // tile_count, width)
    return jnp.take(arrived, proc_order, axis=0).reshape(
        tile_count * tile_local * (TILE_ROWS // tile_count), width
    )


def solution(mesh):
    in_specs = (
        P(("groups", "tile"), None),
        P(("groups", "tile"), None),
        P(),
        P(),
        P(),
        P(),
        P(),
        P(),
        P("groups", None),
        P("groups"),
        P("groups"),
        P("groups"),
    )
    out_specs = P(("groups", "tile"), None)
    return jax.shard_map(local, mesh=mesh, in_specs=in_specs, out_specs=out_specs, check_vma=False)
```

```python
import functools

import jax
import jax.numpy as jnp
from jax import lax
from jax.experimental import pallas as pl
from jax.experimental.pallas import tpu as pltpu
from jax.sharding import PartitionSpec as P

HEADS = 8
BLOCK = 64
NSEL = 32
TILE_ROWS = 128
CHUNK = 512
NEG = -1e30


def attend_kernel(
    owned,
    list_ref,
    count_ref,
    position_ref,
    grid_ref,
    blocks_ref,
    mean_ref,
    rstd_ref,
    w_obs_ref,
    b_obs_ref,
    w_query_ref,
    w_key_ref,
    w_value_ref,
    w_out_ref,
    out_ref,
    raw,
    keys,
    values,
    copy_sem,
):
    tile = pl.program_id(0)
    tiles = pl.num_programs(0)
    key_span = NSEL * BLOCK
    width = grid_ref.shape[1]
    pair = 2 * (width // HEADS)
    base = lax.axis_index("tile") * tiles if owned else 0

    def fetch(which):
        slot = lax.rem(which, 2)

        def one(j, carry):
            spot = position_ref[list_ref[base + which, j]]
            pltpu.make_async_copy(
                blocks_ref.at[pl.ds(spot * BLOCK, BLOCK), :],
                raw.at[slot, pl.ds(j * BLOCK, BLOCK), :],
                copy_sem.at[slot],
            ).start()
            return carry

        lax.fori_loop(0, NSEL, one, 0)

    @pl.when(tile == 0)
    def _():
        fetch(tile)

    slot = lax.rem(tile, 2)
    pltpu.make_async_copy(
        blocks_ref.at[pl.ds(0, key_span), :], raw.at[slot], copy_sem.at[slot]
    ).wait()

    @pl.when(tile + 1 < tiles)
    def _():
        fetch(tile + 1)

    for start in range(0, key_span, CHUNK):
        rows = pl.ds(start, CHUNK)
        feats = raw[slot, rows, :].astype(jnp.float32)
        normed = ((feats - mean_ref[...]) * rstd_ref[...]).astype(jnp.bfloat16)
        hidden = jnp.dot(normed, w_obs_ref[...], preferred_element_type=jnp.float32)
        hidden = hidden + b_obs_ref[...]
        embedded = jax.nn.gelu(hidden, approximate=True).astype(jnp.bfloat16)
        keys[rows, :] = jnp.dot(
            embedded, w_key_ref[...], preferred_element_type=jnp.float32
        ).astype(jnp.bfloat16)
        values[rows, :] = jnp.dot(
            embedded, w_value_ref[...], preferred_element_type=jnp.float32
        ).astype(jnp.bfloat16)

    queries = jnp.dot(
        grid_ref[...], w_query_ref[...], preferred_element_type=jnp.float32
    ).astype(jnp.bfloat16)
    queries = queries * jnp.bfloat16(1.0 / (width // HEADS) ** 0.5)
    certain = 3 * key_span // 4
    used = count_ref[base + tile] * BLOCK
    key_index = certain + lax.broadcasted_iota(jnp.int32, (1, key_span - certain), 1)
    bias = jnp.where(key_index < used, 0.0, NEG).astype(jnp.float32)
    lane = lax.broadcasted_iota(jnp.int32, (TILE_ROWS, pair), 1)
    first = lane < pair // 2
    zero = jnp.zeros((), jnp.bfloat16)
    parts = []
    for p in range(HEADS // 2):
        columns = slice(p * pair, (p + 1) * pair)
        q = queries[:, columns]
        both = jnp.concatenate([jnp.where(first, q, zero), jnp.where(first, zero, q)], axis=0)
        scores = lax.dot_general(
            both,
            keys[:, columns],
            (((1,), (1,)), ((), ())),
            preferred_element_type=jnp.float32,
        )
        scores = jnp.concatenate([scores[:, :certain], scores[:, certain:] + bias], axis=1)
        peak = jnp.max(scores, axis=-1, keepdims=True)
        expo = jnp.exp(scores - peak)
        totals = jnp.sum(expo, axis=-1, keepdims=True)
        mixed = jnp.dot(
            expo.astype(jnp.bfloat16), values[:, columns], preferred_element_type=jnp.float32
        )
        mixed = mixed / totals
        parts.append(
            jnp.where(first, mixed[:TILE_ROWS], mixed[TILE_ROWS:]).astype(jnp.bfloat16)
        )
    attended = jnp.concatenate(parts, axis=1)
    encoded = jnp.dot(
        attended, w_out_ref[...], preferred_element_type=jnp.float32
    ).astype(jnp.bfloat16)
    out_ref[...] = encoded.reshape(out_ref.shape)


def attend(
    tile_count,
    owned,
    lists,
    counts,
    position,
    grid_tokens,
    blocks,
    mean,
    rstd,
    w_obs,
    b_obs,
    w_query,
    w_key,
    w_value,
    w_out,
):
    rows, width = grid_tokens.shape
    piece = TILE_ROWS // tile_count
    feat = blocks.shape[1]
    key_span = NSEL * BLOCK

    def whole(shape):
        return pl.BlockSpec(shape, lambda t, *_: (0, 0))

    square = whole((width, width))
    return pl.pallas_call(
        functools.partial(attend_kernel, owned),
        grid_spec=pltpu.PrefetchScalarGridSpec(
            num_scalar_prefetch=3,
            grid=(rows // TILE_ROWS,),
            in_specs=[
                pl.BlockSpec((TILE_ROWS, width), lambda t, *_: (t, 0)),
                pl.BlockSpec(memory_space=pl.ANY),
                whole((1, feat)),
                whole((1, feat)),
                whole((feat, width)),
                whole((1, width)),
                square,
                square,
                square,
                square,
            ],
            out_specs=pl.BlockSpec((tile_count, 1, piece, width), lambda t, *_: (0, t, 0, 0)),
            scratch_shapes=[
                pltpu.VMEM((2, key_span, feat), jnp.bfloat16),
                pltpu.VMEM((key_span, width), jnp.bfloat16),
                pltpu.VMEM((key_span, width), jnp.bfloat16),
                pltpu.SemaphoreType.DMA((2,)),
            ],
        ),
        out_shape=jax.ShapeDtypeStruct(
            (tile_count, rows // TILE_ROWS, piece, width), jnp.bfloat16
        ),
        compiler_params=pltpu.CompilerParams(dimension_semantics=("arbitrary",)),
        cost_estimate=pl.CostEstimate(
            flops=12_000_000_000, bytes_accessed=6_000_000, transcendentals=12_000_000
        ),
    )(
        lists,
        counts,
        position,
        grid_tokens,
        blocks,
        mean,
        rstd,
        w_obs,
        b_obs[None],
        w_query,
        w_key,
        w_value,
        w_out,
    )


MESH = pl.DeviceIdType.MESH


def greet_all(me, count):
    barrier = pltpu.get_barrier_semaphore()

    def one(k, carry):
        peer = lax.rem(me + k, count)
        pl.semaphore_signal(barrier, inc=1, device_id={"tile": peer}, device_id_type=MESH)
        return carry

    lax.fori_loop(1, count, one, 0)
    pl.semaphore_wait(barrier, count - 1)


def gather_kernel(
    lines, obs_ref, all_ref, mean_ref, rstd_ref, part, parts, sends, recvs, part_sends, part_recvs, own_sem
):
    count = 4 * lines
    me = lax.axis_index("tile")
    z, y, c = me // 4, lax.rem(me // 2, 2), lax.rem(me, 2)
    rows = obs_ref.shape[0]
    half = rows // 2
    odd = lax.rem(z, 2)

    def index(zz, yy, cc):
        return (zz * 2 + yy) * 2 + cc

    down, up = index(z - 1, y, c), index(z + 1, y, c)
    across, beside = index(z, 1 - y, c), index(z, y, 1 - c)
    buddy_z = z + 1 - 2 * odd
    buddy = index(buddy_z, y, c)
    targets = (down, up, across, beside, buddy)

    def place(block, h):
        return all_ref.at[pl.ds(pl.multiple_of(block * rows + h * half, half), half), :]

    def send(block, h, way, own=False):
        return pltpu.make_async_remote_copy(
            src_ref=obs_ref.at[pl.ds(h * half, half), :] if own else place(block, h),
            dst_ref=place(block, h),
            send_sem=sends.at[way, 2 * block + h],
            recv_sem=recvs.at[2 * block + h],
            device_id={"tile": targets[way]},
            device_id_type=MESH,
        )

    greet_all(me, count)
    for h in range(2):

        @pl.when(z > 0)
        def _():
            send(me, h, 0, True).start()

        @pl.when(z < lines - 1)
        def _():
            send(me, h, 1, True).start()

        send(me, h, 2, True).start()
        send(me, h, 3, True).start()
    own = pltpu.make_async_copy(
        obs_ref, all_ref.at[pl.ds(pl.multiple_of(me * rows, rows), rows), :], own_sem
    )
    own.start()

    feats = obs_ref[...].astype(jnp.float32)
    part[...] = jnp.zeros_like(part)
    part[0:1, :] = jnp.sum(feats, axis=0, keepdims=True)
    part[1:2, :] = jnp.sum(feats * feats, axis=0, keepdims=True)
    parts[pl.ds(me, 1)] = part[...][None]

    for hop in range(1, lines + 1):
        for h in range(2):
            if hop < lines:
                from_up, from_down = index(z + hop, y, c), index(z - hop, y, c)

                @pl.when(z + hop < lines)
                def _():
                    send(from_up, h, 3).wait_recv()

                    @pl.when(z > 0)
                    def _():
                        send(from_up, h, 0).start()

                    if hop == 1 and h == 1:

                        @pl.when(odd == 1)
                        def _():
                            send(from_up, h, 2).start()

                    else:
                        send(from_up, h, 2).start()
                    send(from_up, h, 3).start()

                @pl.when(z - hop >= 0)
                def _():
                    send(from_down, h, 3).wait_recv()

                    @pl.when(z < lines - 1)
                    def _():
                        send(from_down, h, 1).start()

                    if hop == 1 and h == 1:

                        @pl.when(odd == 0)
                        def _():
                            send(from_down, h, 2).start()

                    else:
                        send(from_down, h, 2).start()
                    send(from_down, h, 3).start()

            far = hop - 1
            for sign in (1, -1) if far else (1,):
                other = index(z + sign * far, 1 - y, c)

                @pl.when((z + sign * far >= 0) & (z + sign * far < lines))
                def _():
                    send(other, h, 3).wait_recv()
                    if far == 0 and h == 1:
                        send(other, h, 4).start()
                    send(other, h, 3).start()

        if hop == 1:

            def share(k, carry):
                peer = lax.rem(me + k, count)
                pltpu.make_async_remote_copy(
                    src_ref=part,
                    dst_ref=parts.at[me],
                    send_sem=part_sends.at[k],
                    recv_sem=part_recvs.at[me],
                    device_id={"tile": peer},
                    device_id_type=MESH,
                ).start()
                return carry

            lax.fori_loop(1, count, share, 0)

    def gathered(k, carry):
        peer = lax.rem(me + k, count)
        copy = pltpu.make_async_remote_copy(
            src_ref=part,
            dst_ref=parts.at[peer],
            send_sem=part_sends.at[k],
            recv_sem=part_recvs.at[peer],
            device_id={"tile": peer},
            device_id_type=MESH,
        )
        copy.wait_send()
        copy.wait_recv()
        return carry

    lax.fori_loop(1, count, gathered, 0)
    sums = jnp.sum(parts[...], axis=0)
    total = rows * count
    mean = sums[0:1, :] / total
    mean_ref[...] = mean
    rstd_ref[...] = lax.rsqrt(sums[1:2, :] / total - mean * mean + 1e-05)

    for zz in range(lines):
        held = index(zz, y, c)
        for h in range(2):
            for yy in range(2):
                send(index(zz, yy, 1 - c), h, 3).wait_recv()
                send(index(zz, yy, c), h, 3).wait_send()
            if h == 1:

                @pl.when(buddy_z != zz)
                def _():
                    send(held, h, 2).wait_send()

            else:
                send(held, h, 2).wait_send()

            @pl.when((zz >= z) & (z > 0))
            def _():
                send(held, h, 0).wait_send()

            @pl.when((zz <= z) & (z < lines - 1))
            def _():
                send(held, h, 1).wait_send()

    send(across, 1, 4).wait_send()
    own.wait()


def gather_blocks(obs_features, tile_count):
    rows, feat = obs_features.shape
    small = jax.ShapeDtypeStruct((1, feat), jnp.float32)
    vmem = pl.BlockSpec(memory_space=pltpu.VMEM)
    return pl.pallas_call(
        functools.partial(gather_kernel, tile_count // 4),
        out_shape=(
            jax.ShapeDtypeStruct((tile_count * rows, feat), obs_features.dtype),
            small,
            small,
        ),
        in_specs=[vmem],
        out_specs=(pl.BlockSpec(memory_space=pl.ANY), vmem, vmem),
        scratch_shapes=[
            pltpu.VMEM((8, feat), jnp.float32),
            pltpu.VMEM((tile_count, 8, feat), jnp.float32),
            pltpu.SemaphoreType.DMA((5, 2 * tile_count)),
            pltpu.SemaphoreType.DMA((2 * tile_count,)),
            pltpu.SemaphoreType.DMA((tile_count,)),
            pltpu.SemaphoreType.DMA((tile_count,)),
            pltpu.SemaphoreType.DMA,
        ],
        compiler_params=pltpu.CompilerParams(collective_id=0, has_side_effects=True),
    )(obs_features)


def scatter_kernel(count, order_ref, encoded_ref, out_ref, arrived, sends, recvs):
    me = lax.axis_index("tile")
    tile_local = encoded_ref.shape[1]
    greet_all(me, count)

    def copy(source, peer, k):
        return pltpu.make_async_remote_copy(
            src_ref=encoded_ref.at[peer],
            dst_ref=arrived.at[pl.ds(source * tile_local, tile_local)],
            send_sem=sends.at[k],
            recv_sem=recvs.at[source],
            device_id={"tile": peer},
            device_id_type=MESH,
        )

    def start(k, carry):
        copy(me, lax.rem(me + k, count), k).start()
        return carry

    def finish(k, carry):
        peer = lax.rem(me + k, count)
        copy(peer, peer, k).wait_send()
        copy(peer, peer, k).wait_recv()
        return carry

    lax.fori_loop(1, count, start, 0)
    arrived[pl.ds(me * tile_local, tile_local)] = encoded_ref[me]
    lax.fori_loop(1, count, finish, 0)

    def arrange(j, carry):
        out_ref[pl.ds(j, 1)] = arrived[pl.ds(order_ref[j], 1)]
        return carry

    lax.fori_loop(0, count * tile_local, arrange, 0, unroll=8)


def scatter(encoded, proc_order):
    count, tile_local, piece, width = encoded.shape
    vmem = pl.BlockSpec(memory_space=pltpu.VMEM)
    shape = (count * tile_local, piece, width)
    return pl.pallas_call(
        functools.partial(scatter_kernel, count),
        out_shape=jax.ShapeDtypeStruct(shape, encoded.dtype),
        in_specs=[pl.BlockSpec(memory_space=pltpu.SMEM), vmem],
        out_specs=vmem,
        scratch_shapes=[
            pltpu.VMEM(shape, encoded.dtype),
            pltpu.SemaphoreType.DMA((count,)),
            pltpu.SemaphoreType.DMA((count,)),
        ],
        compiler_params=pltpu.CompilerParams(collective_id=1, has_side_effects=True),
    )(proc_order, encoded).reshape(count * tile_local * piece, width)


def exchange(obs_features, block_lists, block_counts, block_position, tile_count, own_index):
    obs_blocks = obs_features.shape[0] // BLOCK
    tile_local = block_lists.shape[0] // tile_count
    entry_count = tile_local * NSEL
    capacity = max(2, 2 * entry_count // tile_count)
    spots = jnp.take(block_position, block_lists, axis=0)
    is_valid = jnp.arange(NSEL, dtype=jnp.int32)[None, :] < block_counts[:, None]
    owner_dev = (spots // obs_blocks).reshape(tile_count, entry_count)
    local_blk = (spots % obs_blocks).reshape(tile_count, entry_count)
    valid_rows = is_valid.reshape(tile_count, entry_count)
    entry_order = jnp.arange(entry_count, dtype=jnp.int32)
    earlier = (
        (owner_dev[:, :, None] == owner_dev[:, None, :])
        & valid_rows[:, None, :]
        & (entry_order[None, :] < entry_order[:, None])[None, :, :]
    )
    slot_rank = jnp.sum(earlier.astype(jnp.int32), axis=2)
    mine = valid_rows & (owner_dev == own_index)
    slot_ids = jnp.arange(capacity, dtype=jnp.int32)
    hits = mine[:, None, :] & (slot_rank[:, None, :] == slot_ids[None, :, None])
    slot_block = jnp.sum(jnp.where(hits, local_blk[:, None, :], 0), axis=2)
    my_owner = lax.dynamic_index_in_dim(owner_dev, own_index, 0, keepdims=False)
    my_rank = lax.dynamic_index_in_dim(slot_rank, own_index, 0, keepdims=False)
    my_valid = lax.dynamic_index_in_dim(valid_rows, own_index, 0, keepdims=False)
    pick = jnp.where(my_valid, my_owner * capacity + my_rank, 0)
    raw_blocks = obs_features.reshape(obs_blocks, BLOCK, obs_features.shape[1])
    incoming = lax.all_to_all(
        jnp.take(raw_blocks, slot_block, axis=0), "tile", split_axis=0, concat_axis=0, tiled=True
    )
    return incoming.reshape(tile_count * capacity * BLOCK, obs_features.shape[1]), pick


def local(
    grid_tokens,
    obs_features,
    w_obs,
    b_obs,
    w_query,
    w_key,
    w_value,
    w_out,
    block_lists,
    block_counts,
    block_position,
    proc_order,
):
    tile_count = lax.axis_size("tile")
    own_index = lax.axis_index("tile")
    tile_local = grid_tokens.shape[0] // TILE_ROWS
    width = grid_tokens.shape[1]
    near = tile_count <= 16 and tile_count % 8 == 0
    if near:
        blocks, feat_mean, feat_rstd = gather_blocks(obs_features, tile_count)
        lists, counts, position = block_lists, block_counts, block_position
    else:
        obs_wide = obs_features.astype(jnp.float32)
        first_sum, second_sum = lax.psum(
            (
                jnp.sum(obs_wide, axis=0, keepdims=True),
                jnp.sum(obs_wide * obs_wide, axis=0, keepdims=True),
            ),
            "tile",
        )
        obs_total = obs_features.shape[0] * tile_count
        feat_mean = first_sum / obs_total
        feat_rstd = lax.rsqrt(second_sum / obs_total - feat_mean * feat_mean + 1e-05)
        blocks, pick = exchange(
            obs_features, block_lists, block_counts, block_position, tile_count, own_index
        )
        lists = pick.reshape(tile_local, NSEL)
        counts = lax.dynamic_slice_in_dim(block_counts, own_index * tile_local, tile_local)
        position = jnp.arange(blocks.shape[0] // BLOCK, dtype=jnp.int32)
    encoded = attend(
        tile_count if near else 1,
        near,
        lists,
        counts,
        position,
        grid_tokens,
        blocks,
        feat_mean,
        feat_rstd,
        w_obs,
        b_obs,
        w_query,
        w_key,
        w_value,
        w_out,
    )
    if near:
        return scatter(encoded, proc_order)
    outgoing = encoded.reshape(tile_local, tile_count, TILE_ROWS // tile_count, width)
    arrived = lax.all_to_all(outgoing, "tile", split_axis=1, concat_axis=0, tiled=True)
    arrived = arrived.reshape(tile_count * tile_local, TILE_ROWS // tile_count, width)
    return jnp.take(arrived, proc_order, axis=0).reshape(
        tile_count * tile_local * (TILE_ROWS // tile_count), width
    )


def solution(mesh):
    in_specs = (
        P(("groups", "tile"), None),
        P(("groups", "tile"), None),
        P(),
        P(),
        P(),
        P(),
        P(),
        P(),
        P("groups", None),
        P("groups"),
        P("groups"),
        P("groups"),
    )
    out_specs = P(("groups", "tile"), None)
    return jax.shard_map(local, mesh=mesh, in_specs=in_specs, out_specs=out_specs, check_vma=False)
```
